512 devices in a mesh: src: 16 (over y_hi, x, core), rcv: 32 (over y_lo, z).
Axes of the slice: x: 4, y: 4 (y_hi: 2, y_lo: 2; y = y_hi * 2 + y_lo), z: 16, core: 2. Of those that a mesh axis runs over, the one named last changes fastest.
Arguments:
- spectra: bfloat16 [2, 8, 192, 8192], P(None, None, 'src', 'rcv'), as said below
- alive: int32 [192, 8192], P('src', 'rcv'), may hold values 0 or 1
Outputs:
- stacked: bfloat16 [2, 8, 8192, 8192], P(None, None, 'src', 'rcv')
The draws below stay inside these ranges and needn't reach their ends.
Inputs may be any that keep to these rules, and one draw needn't show every extreme that they name: spectra: every entry is a random factor times an amplitude of its window and channel that spreads over a factor of 15.
All inputs are finite; a program needn't handle non-finite values. No bound on the sum of `alive` on one device may be relied on, other than what follows from the above.
Results may differ from the reference program's by a relative error of at most 0.0057.
Values may be sent and summed in bfloat16 or wider, within the bound.
No kernel may reach another device: no remote copies, remote signals or barrier semaphores. Data moves between devices by JAX's collectives and lax.ppermute only.
A program may use at most 64 MiB of HBM per device.

```python
import math
import jax
import jax.numpy as jnp
from jax import lax

BINS = 8
WINDOWS = 192
CHANNELS = 8192


def draw_spectra(key, part):
    key_amp = jax.random.fold_in(key, 11)
    key_base = jax.random.fold_in(key, 23)
    amplitude = jnp.exp(jax.random.uniform(key_amp, (1, 1, WINDOWS, CHANNELS), jnp.float32, math.log(0.2), math.log(3.0)))
    base = jax.random.normal(key_base, (2, BINS, WINDOWS, CHANNELS), jnp.float32)
    return (base * amplitude).astype(jnp.bfloat16)


def set_ends(entries, stream_key, least, largest):
    index_at = [jax.random.randint(jax.random.fold_in(stream_key, axis), (), 0, length) for axis, length in enumerate(entries.shape)]
    main_axis = entries.shape.index(max(entries.shape))
    neighbour = index_at[:main_axis] + [(index_at[main_axis] + 1) % entries.shape[main_axis]] + index_at[main_axis + 1:]
    return entries.at[tuple(index_at)].set(least).at[tuple(neighbour)].set(largest)


def setup_inputs(seed: int = 0) -> dict:
    streams_of = jax.random.split(jax.random.key(seed), 3)
    spectra = draw_spectra(jax.random.fold_in(streams_of[2], 71), 0)
    alive = set_ends((jax.random.randint(streams_of[1], (WINDOWS, CHANNELS), 0, 8) < 7).astype(jnp.int32), jax.random.fold_in(streams_of[1], 1), 0, 1)
    return dict(spectra=spectra, alive=alive)


def whiten(spectra, alive):
    values = spectra.astype(jnp.float32)
    power = lax.optimization_barrier(jnp.sum(values * values, axis=(0, 1))) / BINS
    factor = alive.astype(jnp.float32) / jnp.sqrt(jnp.maximum(power, 0.5))
    return (values * factor).astype(jnp.bfloat16)

def one_bin(pair):
    real_part = pair[0]
    imag_part = pair[1]
    first = jnp.dot(real_part.T, real_part, preferred_element_type=jnp.float32)
    second = jnp.dot(imag_part.T, imag_part, preferred_element_type=jnp.float32)
    third = jnp.dot(real_part.T, imag_part, preferred_element_type=jnp.float32)
    fourth = jnp.dot(imag_part.T, real_part, preferred_element_type=jnp.float32)
    return (first + second, third - fourth)

def reference(spectra, alive):
    whitened = whiten(spectra, alive)
    by_bin = jnp.moveaxis(whitened, 1, 0)
    real_stack, imag_stack = lax.map(one_bin, by_bin)
    factor = jnp.float32(1.0) / jnp.sqrt(jnp.float32(WINDOWS))
    return (jnp.stack((real_stack, imag_stack)) * factor).astype(jnp.bfloat16)
```

```python
import jax
import jax.numpy as jnp
import numpy as np
from jax import lax
from jax.experimental import pallas as pl
from jax.experimental.pallas import tpu as pltpu
from jax.sharding import PartitionSpec as P

OWN_SLOTS = ((0, -5, 5), (-1, -6, 4), (1, -4, 6), (-2, -7, 3), (2, -3, 7), (8,))
NEIGHBOUR_SLOTS = ((0, -5, 5), (-1, -6, 4), (1, -4, 6), (-2, -7, 3), (2, -3, 7, 8))


def whiten_kernel(bins, spectra_ref, alive_ref, out_ref, rows_ref):
    windows = spectra_ref.shape[1]
    for window in range(windows):
        real = spectra_ref[0, window].astype(jnp.float32)
        imag = spectra_ref[1, window].astype(jnp.float32)
        power = jnp.sum(real * real + imag * imag, axis=0, keepdims=True) / bins
        live = alive_ref[window : window + 1, :].astype(jnp.float32)
        factor = live / jnp.sqrt(jnp.maximum(power, 0.5))
        rows_ref[0, window] = real * factor
        rows_ref[1, window] = imag * factor
    values = rows_ref[...].reshape(2 * windows, bins, rows_ref.shape[-1])
    out_ref[...] = jnp.swapaxes(values, 0, 1).astype(jnp.bfloat16)


def whiten(spectra, alive):
    _, bins, windows, channels = spectra.shape
    by_window = jnp.swapaxes(spectra, 1, 2)
    return pl.pallas_call(
        lambda *refs: whiten_kernel(bins, *refs),
        out_shape=jax.ShapeDtypeStruct((bins, 2 * windows, channels), jnp.bfloat16),
        scratch_shapes=[pltpu.VMEM((2, windows, bins, channels), jnp.float32)],
        name="whiten",
    )(by_window, alive)


def receiver_kernel(in_ref, out_ref):
    slices, _, rows, channels = in_ref.shape
    for piece in range(slices):
        block = in_ref[piece, 0]
        wide = block.astype(jnp.float32)
        turned = jnp.concatenate((wide[rows // 2 :], -wide[: rows // 2]), axis=0)
        out_ref[0, piece, :, :channels] = block
        out_ref[0, piece, :, channels:] = turned.astype(jnp.bfloat16)


def receiver_pairs(receivers):
    slices, bins, rows, channels = receivers.shape
    return pl.pallas_call(
        receiver_kernel,
        grid=(bins,),
        in_specs=[pl.BlockSpec((slices, 1, rows, channels), lambda f: (0, f, 0, 0))],
        out_specs=pl.BlockSpec((1, slices, rows, 2 * channels), lambda f: (f, 0, 0, 0)),
        out_shape=jax.ShapeDtypeStruct((bins, slices, rows, 2 * channels), jnp.bfloat16),
        name="receiver_pairs",
    )(receivers)


def stack_kernel(parities, scale, place_ref, *refs):
    groups = refs[: len(parities)]
    pairs_ref, out_ref, even_ref, odd_ref = refs[len(parities) :]
    rows = groups[0].shape[2]
    channels = groups[0].shape[3]
    slot = 0
    for group, parity in zip(groups, parities):
        for i in range(group.shape[0]):
            held = odd_ref if parity[i] else even_ref
            held[place_ref[slot]] = group[i, 0]
            slot += 1
    pairs = pairs_ref[0].reshape(-1, 2 * channels)
    for held, side in ((even_ref, place_ref[slot]), (odd_ref, 1 - place_ref[slot])):
        total = lax.dot_general(
            held[...].reshape(-1, channels),
            pairs,
            (((0,), (0,)), ((), ())),
            preferred_element_type=jnp.float32,
        )
        total = (total * scale).astype(jnp.bfloat16)
        at = pl.ds(pl.multiple_of(side * channels, channels), channels)
        out_ref[0, 0, at, :] = total[:, :channels]
        out_ref[1, 0, at, :] = total[:, channels:]


def stack(groups, parities, place, pairs, scale):
    bins, slices, rows, twice = pairs.shape
    channels = twice // 2
    return pl.pallas_call(
        lambda *refs: stack_kernel(parities, scale, *refs),
        grid=(bins,),
        in_specs=[pl.BlockSpec(memory_space=pltpu.SMEM)]
        + [pl.BlockSpec((g.shape[0], 1, rows, channels), lambda f: (0, f, 0, 0)) for g in groups]
        + [pl.BlockSpec((1, slices, rows, twice), lambda f: (f, 0, 0, 0))],
        out_specs=pl.BlockSpec((2, 1, 2 * channels, channels), lambda f: (0, f, 0, 0)),
        out_shape=jax.ShapeDtypeStruct((2, bins, 2 * channels, channels), jnp.bfloat16),
        scratch_shapes=[pltpu.VMEM((slices, rows, channels), jnp.bfloat16)] * 2,
        name="stack",
    )(place, *groups, pairs)


def body(spectra, alive):
    rows_n, cols_n = lax.axis_size("src"), lax.axis_size("rcv")
    length = cols_n // 2
    windows = spectra.shape[2] * rows_n

    def along(z_of, step):
        return z_of // length * length + (z_of % length + step) % length

    def shift(block, step):
        return lax.ppermute(block, "rcv", [(r, along(r, step)) for r in range(cols_n)])

    def trade(block):
        return lax.ppermute(block, "rcv", [(r, (r + length) % cols_n) for r in range(cols_n)])

    def deal(block, step):
        pairs = [
            (s * cols_n + 2 * d + o, d * cols_n + along(2 * s + o, step))
            for s in range(rows_n)
            for d in range(rows_n)
            for o in range(2)
        ]
        return lax.ppermute(block, ("src", "rcv"), pairs)

    local = whiten(spectra, alive)
    dealt = [deal(local, step)[None] for step in (0, 5, -5)]
    receivers = lax.all_to_all(
        jnp.broadcast_to(local[None], (rows_n,) + local.shape), "src", 0, 0
    )
    *dealt, receivers = lax.optimization_barrier((*dealt, receivers))
    first = jnp.concatenate(dealt, axis=0)
    up, down, other = shift(first, 1), shift(first, -1), trade(first)
    up2, down2, far = shift(up, 1), shift(down, -1), shift(down[2:], -2)
    other_up, other_down = shift(other, 1), shift(other, -1)
    other_up2 = shift(other_up, 1)
    last = trade(jnp.concatenate((down2, far), axis=0))
    pairs = receiver_pairs(receivers)

    groups = (first, up, down, up2, down2, far, other, other_up, other_down, other_up2, last)
    own = lax.axis_index("rcv") // length
    z = lax.axis_index("rcv") % length
    offsets = OWN_SLOTS + NEIGHBOUR_SLOTS
    swaps = [i >= len(OWN_SLOTS) for i, group in enumerate(offsets) for _ in group]
    steps = [step % length for group in offsets for step in group]
    row = jnp.where(np.array(swaps), 1 - own, own)
    place = row * (rows_n // 2) + lax.rem(z + np.array(steps, np.int32), length) // 2
    place = jnp.append(place, z % 2).astype(jnp.int32)
    parities = tuple(tuple(step % 2 for step in group) for group in offsets)
    scale = 1.0 / float(windows) ** 0.5
    return stack(groups, parities, place, pairs, scale)


def solution(mesh):
    return jax.shard_map(
        body,
        mesh=mesh,
        in_specs=(P(None, None, "src", "rcv"), P("src", "rcv")),
        out_specs=P(None, None, "src", "rcv"),
        check_vma=False,
    )
```

```python
import jax
import jax.numpy as jnp
import numpy as np
from jax import lax
from jax.experimental import pallas as pl
from jax.experimental.pallas import tpu as pltpu
from jax.sharding import PartitionSpec as P

TILE = 8
STEP = 2

OWN_SLOTS = ((0, -5, 5), (-1, -6, 4), (1, -4, 6), (-2, -7, 3), (2, -3, 7), (8,))
NEIGHBOUR_SLOTS = ((0, -5, 5), (-1, -6, 4), (1, -4, 6), (-2, -7, 3), (2, -3, 7, 8))


def row_of(part, window, windows):
    head = windows // TILE * TILE
    if window < head:
        return part * (2 * windows - head) + window
    return head + part * (windows - head) + window - head


def whiten_kernel(bins, spectra_ref, alive_ref, out_ref, copies_ref, rows_ref):
    windows = spectra_ref.shape[1]
    for window in range(windows):
        real = spectra_ref[0, window].astype(jnp.float32)
        imag = spectra_ref[1, window].astype(jnp.float32)
        power = jnp.sum(real * real + imag * imag, axis=0, keepdims=True) / bins
        live = alive_ref[window : window + 1, :].astype(jnp.float32)
        factor = live / jnp.sqrt(jnp.maximum(power, 0.5))
        rows_ref[row_of(0, window, windows)] = real * factor
        rows_ref[row_of(1, window, windows)] = imag * factor
    out_ref[...] = jnp.swapaxes(rows_ref[...], 0, 1).astype(jnp.bfloat16)
    for i in range(copies_ref.shape[0]):
        copies_ref[i] = out_ref[...]


def whiten(spectra, alive, copies):
    _, bins, windows, channels = spectra.shape
    by_window = jnp.swapaxes(spectra, 1, 2)
    return pl.pallas_call(
        lambda *refs: whiten_kernel(bins, *refs),
        out_shape=(
            jax.ShapeDtypeStruct((bins, 2 * windows, channels), jnp.bfloat16),
            jax.ShapeDtypeStruct((copies, bins, 2 * windows, channels), jnp.bfloat16),
        ),
        scratch_shapes=[pltpu.VMEM((2 * windows, bins, channels), jnp.float32)],
        name="whiten",
    )(by_window, alive)


def receiver_kernel(*refs):
    *in_refs, out_ref = refs
    slices, bins, rows, channels = in_refs[0].shape
    head = rows // 2 // TILE * TILE
    tail = rows - head
    half = (tail - head) // 2
    for f in range(bins):
        for piece in range(slices * len(in_refs)):
            block = in_refs[piece // slices][piece % slices, f]
            out_ref[f, piece, :, :channels] = block
            out_ref[f, piece, :head, channels:] = block[tail:]
            out_ref[f, piece, tail:, channels:] = -block[:head]
            mixed = block[head:tail].astype(jnp.float32)
            turned = jnp.concatenate((mixed[half:], -mixed[:half]), axis=0)
            out_ref[f, piece, head:tail, channels:] = turned.astype(jnp.bfloat16)


def receiver_pairs(receivers):
    slices, bins, rows, channels = receivers[0].shape
    total = slices * len(receivers)
    return pl.pallas_call(
        receiver_kernel,
        grid=(bins // STEP,),
        in_specs=[pl.BlockSpec((slices, STEP, rows, channels), lambda f: (0, f, 0, 0))] * len(receivers),
        out_specs=pl.BlockSpec((STEP, total, rows, 2 * channels), lambda f: (f, 0, 0, 0)),
        out_shape=jax.ShapeDtypeStruct((bins, total, rows, 2 * channels), jnp.bfloat16),
        name="receiver_pairs",
    )(*receivers)


def stack_kernel(parities, scale, place_ref, *refs):
    groups = refs[: len(parities)]
    pairs_ref, out_ref, even_ref, odd_ref = refs[len(parities) :]
    channels = groups[0].shape[3]
    parity_at = sum(group.shape[0] for group in groups)
    for f in range(out_ref.shape[1]):
        slot = 0
        for group, parity in zip(groups, parities):
            for i in range(group.shape[0]):
                held = odd_ref if parity[i] else even_ref
                held[f, place_ref[slot]] = group[i, f]
                slot += 1
        pairs = pairs_ref[f].reshape(-1, 2 * channels)
        for held, side in ((even_ref, place_ref[parity_at]), (odd_ref, 1 - place_ref[parity_at])):
            total = lax.dot_general(
                held[f].reshape(-1, channels),
                pairs,
                (((0,), (0,)), ((), ())),
                preferred_element_type=jnp.float32,
            )
            total = (total * scale).astype(jnp.bfloat16)
            at = pl.ds(pl.multiple_of(side * channels, channels), channels)
            out_ref[0, f, at, :] = total[:, :channels]
            out_ref[1, f, at, :] = total[:, channels:]


def stack(groups, parities, place, pairs, scale):
    bins, slices, rows, twice = pairs.shape
    channels = twice // 2
    return pl.pallas_call(
        lambda *refs: stack_kernel(parities, scale, *refs),
        grid=(bins // STEP,),
        in_specs=[pl.BlockSpec(memory_space=pltpu.SMEM)]
        + [pl.BlockSpec((g.shape[0], STEP, rows, channels), lambda f: (0, f, 0, 0)) for g in groups]
        + [pl.BlockSpec((STEP, slices, rows, twice), lambda f: (f, 0, 0, 0))],
        out_specs=pl.BlockSpec((2, STEP, 2 * channels, channels), lambda f: (0, f, 0, 0)),
        out_shape=jax.ShapeDtypeStruct((2, bins, 2 * channels, channels), jnp.bfloat16),
        scratch_shapes=[pltpu.VMEM((STEP, slices, rows, channels), jnp.bfloat16)] * 2,
        name="stack",
    )(place, *groups, pairs)


def body(spectra, alive):
    rows_n, cols_n = lax.axis_size("src"), lax.axis_size("rcv")
    length = cols_n // 2
    windows = spectra.shape[2] * rows_n

    def along(z_of, step):
        return z_of // length * length + (z_of % length + step) % length

    def shift(block, step):
        return lax.ppermute(block, "rcv", [(r, along(r, step)) for r in range(cols_n)])

    def trade(block):
        return lax.ppermute(block, "rcv", [(r, (r + length) % cols_n) for r in range(cols_n)])

    def deal(block, step):
        pairs = [
            (s * cols_n + 2 * d + o, d * cols_n + along(2 * s + o, step))
            for s in range(rows_n)
            for d in range(rows_n)
            for o in range(2)
        ]
        return lax.ppermute(block, ("src", "rcv"), pairs)

    def cross(block, bit):
        return lax.ppermute(block, "src", [(s, s ^ bit) for s in range(rows_n)])

    local, copies = whiten(spectra, alive, rows_n)
    dealt = [deal(local, step)[None] for step in (0, 5, -5)]
    receivers = (lax.all_to_all(copies, "src", 0, 0),)
    first = jnp.concatenate(dealt, axis=0)
    up, down, other = shift(first, 1), shift(first, -1), trade(first)
    up2, down2, far = shift(up, 1), shift(down, -1), shift(down[2:], -2)
    far, pairs = lax.optimization_barrier((far, receiver_pairs(receivers)))
    other_up, other_down = shift(other, 1), shift(other, -1)
    other_up2 = trade(up2)
    last = trade(jnp.concatenate((down2, far), axis=0))

    groups = (first, up, down, up2, down2, far, other, other_up, other_down, other_up2, last)
    own = lax.axis_index("rcv") // length
    z = lax.axis_index("rcv") % length
    offsets = OWN_SLOTS + NEIGHBOUR_SLOTS
    swaps = [i >= len(OWN_SLOTS) for i, group in enumerate(offsets) for _ in group]
    steps = [step % length for group in offsets for step in group]
    row = jnp.where(np.array(swaps), 1 - own, own)
    place = row * (rows_n // 2) + lax.rem(z + np.array(steps, np.int32), length) // 2
    place = jnp.append(place, z % 2).astype(jnp.int32)
    parities = tuple(tuple(step % 2 for step in group) for group in offsets)
    scale = 1.0 / float(windows) ** 0.5
    return stack(groups, parities, place, pairs, scale)


def solution(mesh):
    return jax.shard_map(
        body,
        mesh=mesh,
        in_specs=(P(None, None, "src", "rcv"), P("src", "rcv")),
        out_specs=P(None, None, "src", "rcv"),
        check_vma=False,
    )
```

```python
import jax
import jax.numpy as jnp
import numpy as np
from jax import lax
from jax.experimental import pallas as pl
from jax.experimental.pallas import tpu as pltpu
from jax.sharding import PartitionSpec as P

TILE = 8
STACK_STEP = 4
STEP = 2

OWN_SLOTS = ((0, -5, 5), (-1, -6, 4), (1, -4, 6), (-2, -7, 3), (2, -3, 7), (8,))
NEIGHBOUR_SLOTS = ((0, -5, 5), (-1, -6, 4), (1, -4, 6), (-2, -7, 3), (2, -3, 7, 8))


def row_of(part, window, windows):
    head = windows // TILE * TILE
    if window < head:
        return part * (2 * windows - head) + window
    return head + part * (windows - head) + window - head


def whiten_kernel(bins, spectra_ref, alive_ref, out_ref, copies_ref, rows_ref):
    windows = spectra_ref.shape[1]
    for window in range(windows):
        real = spectra_ref[0, window].astype(jnp.float32)
        imag = spectra_ref[1, window].astype(jnp.float32)
        power = jnp.sum(real * real + imag * imag, axis=0, keepdims=True) / bins
        live = alive_ref[window : window + 1, :].astype(jnp.float32)
        factor = live / jnp.sqrt(jnp.maximum(power, 0.5))
        rows_ref[row_of(0, window, windows)] = real * factor
        rows_ref[row_of(1, window, windows)] = imag * factor
    out_ref[...] = jnp.swapaxes(rows_ref[...], 0, 1).astype(jnp.bfloat16)
    for i in range(copies_ref.shape[0]):
        copies_ref[i] = out_ref[...]


def whiten(spectra, alive, copies):
    _, bins, windows, channels = spectra.shape
    by_window = jnp.swapaxes(spectra, 1, 2)
    return pl.pallas_call(
        lambda *refs: whiten_kernel(bins, *refs),
        out_shape=(
            jax.ShapeDtypeStruct((bins, 2 * windows, channels), jnp.bfloat16),
            jax.ShapeDtypeStruct((copies, bins, 2 * windows, channels), jnp.bfloat16),
        ),
        scratch_shapes=[pltpu.VMEM((2 * windows, bins, channels), jnp.float32)],
        name="whiten",
    )(by_window, alive)


def receiver_kernel(*refs):
    *in_refs, out_ref = refs
    slices, bins, rows, channels = in_refs[0].shape
    head = rows // 2 // TILE * TILE
    tail = rows - head
    half = (tail - head) // 2
    for f in range(bins):
        for piece in range(slices * len(in_refs)):
            block = in_refs[piece // slices][piece % slices, f]
            out_ref[f, piece, :, :channels] = block
            out_ref[f, piece, :head, channels:] = block[tail:]
            out_ref[f, piece, tail:, channels:] = -block[:head]
            mixed = block[head:tail].astype(jnp.float32)
            turned = jnp.concatenate((mixed[half:], -mixed[:half]), axis=0)
            out_ref[f, piece, head:tail, channels:] = turned.astype(jnp.bfloat16)


def receiver_pairs(receivers):
    slices, bins, rows, channels = receivers[0].shape
    total = slices * len(receivers)
    return pl.pallas_call(
        receiver_kernel,
        grid=(bins // STEP,),
        in_specs=[pl.BlockSpec((slices, STEP, rows, channels), lambda f: (0, f, 0, 0))] * len(receivers),
        out_specs=pl.BlockSpec((STEP, total, rows, 2 * channels), lambda f: (f, 0, 0, 0)),
        out_shape=jax.ShapeDtypeStruct((bins, total, rows, 2 * channels), jnp.bfloat16),
        name="receiver_pairs",
    )(*receivers)


def stack_kernel(parities, scale, place_ref, *refs):
    groups = refs[: len(parities)]
    pairs_ref, out_ref, even_ref, odd_ref = refs[len(parities) :]
    channels = groups[0].shape[3]
    parity_at = sum(group.shape[0] for group in groups)
    for f in range(out_ref.shape[1]):
        slot = 0
        for group, parity in zip(groups, parities):
            for i in range(group.shape[0]):
                held = odd_ref if parity[i] else even_ref
                held[f, place_ref[slot]] = group[i, f]
                slot += 1
        pairs = pairs_ref[f].reshape(-1, 2 * channels)
        for held, side in ((even_ref, place_ref[parity_at]), (odd_ref, 1 - place_ref[parity_at])):
            total = lax.dot_general(
                held[f].reshape(-1, channels),
                pairs,
                (((0,), (0,)), ((), ())),
                preferred_element_type=jnp.float32,
            )
            total = (total * scale).astype(jnp.bfloat16)
            at = pl.ds(pl.multiple_of(side * channels, channels), channels)
            out_ref[0, f, at, :] = total[:, :channels]
            out_ref[1, f, at, :] = total[:, channels:]


def stack(groups, parities, place, pairs, scale):
    bins, slices, rows, twice = pairs.shape
    channels = twice // 2
    return pl.pallas_call(
        lambda *refs: stack_kernel(parities, scale, *refs),
        grid=(bins // STACK_STEP,),
        in_specs=[pl.BlockSpec(memory_space=pltpu.SMEM)]
        + [pl.BlockSpec((g.shape[0], STACK_STEP, rows, channels), lambda f: (0, f, 0, 0)) for g in groups]
        + [pl.BlockSpec((STACK_STEP, slices, rows, twice), lambda f: (f, 0, 0, 0))],
        out_specs=pl.BlockSpec((2, STACK_STEP, 2 * channels, channels), lambda f: (0, f, 0, 0)),
        out_shape=jax.ShapeDtypeStruct((2, bins, 2 * channels, channels), jnp.bfloat16),
        scratch_shapes=[pltpu.VMEM((STACK_STEP, slices, rows, channels), jnp.bfloat16)] * 2,
        name="stack",
    )(place, *groups, pairs)


def body(spectra, alive):
    rows_n, cols_n = lax.axis_size("src"), lax.axis_size("rcv")
    length = cols_n // 2
    windows = spectra.shape[2] * rows_n

    def along(z_of, step):
        return z_of // length * length + (z_of % length + step) % length

    def shift(block, step):
        return lax.ppermute(block, "rcv", [(r, along(r, step)) for r in range(cols_n)])

    def trade(block):
        return lax.ppermute(block, "rcv", [(r, (r + length) % cols_n) for r in range(cols_n)])

    def deal(block, step):
        pairs = [
            (s * cols_n + 2 * d + o, d * cols_n + along(2 * s + o, step))
            for s in range(rows_n)
            for d in range(rows_n)
            for o in range(2)
        ]
        return lax.ppermute(block, ("src", "rcv"), pairs)

    def cross(block, bit):
        return lax.ppermute(block, "src", [(s, s ^ bit) for s in range(rows_n)])

    local, copies = whiten(spectra, alive, rows_n)
    dealt = [deal(local, step)[None] for step in (0, 5, -5)]
    receivers = (lax.all_to_all(copies, "src", 0, 0),)
    first = jnp.concatenate(dealt, axis=0)
    up, down, other = shift(first, 1), shift(first, -1), trade(first)
    up2, down2, far = shift(up, 1), shift(down, -1), shift(down[2:], -2)
    far, pairs = lax.optimization_barrier((far, receiver_pairs(receivers)))
    other_up, other_down = shift(other, 1), shift(other, -1)
    other_up2 = trade(up2)
    last = trade(jnp.concatenate((down2, far), axis=0))

    groups = (first, up, down, up2, down2, far, other, other_up, other_down, other_up2, last)
    own = lax.axis_index("rcv") // length
    z = lax.axis_index("rcv") % length
    offsets = OWN_SLOTS + NEIGHBOUR_SLOTS
    swaps = [i >= len(OWN_SLOTS) for i, group in enumerate(offsets) for _ in group]
    steps = [step % length for group in offsets for step in group]
    row = jnp.where(np.array(swaps), 1 - own, own)
    place = row * (rows_n // 2) + lax.rem(z + np.array(steps, np.int32), length) // 2
    place = jnp.append(place, z % 2).astype(jnp.int32)
    parities = tuple(tuple(step % 2 for step in group) for group in offsets)
    scale = 1.0 / float(windows) ** 0.5
    return stack(groups, parities, place, pairs, scale)


def solution(mesh):
    return jax.shard_map(
        body,
        mesh=mesh,
        in_specs=(P(None, None, "src", "rcv"), P("src", "rcv")),
        out_specs=P(None, None, "src", "rcv"),
        check_vma=False,
    )
```

```python
import jax
import jax.numpy as jnp
import numpy as np
from jax import lax
from jax.experimental import pallas as pl
from jax.experimental.pallas import tpu as pltpu
from jax.sharding import PartitionSpec as P

TILE = 8
STACK_STEP = 4
STEP = 2

OWN_SLOTS = ((0, -5, 5), (-1, -6, 4), (1, -4, 6), (-2, -7, 3), (2, -3, 7), (8,))
NEIGHBOUR_SLOTS = ((0, -5, 5), (-1, -6, 4), (1, -4, 6), (-2, -7, 3, 8), (2, -3, 7))


def row_of(part, window, windows):
    head = windows // TILE * TILE
    if window < head:
        return part * (2 * windows - head) + window
    return head + part * (windows - head) + window - head


def whiten_kernel(bins, spectra_ref, alive_ref, out_ref, copies_ref, rows_ref):
    windows = spectra_ref.shape[1]
    for window in range(windows):
        real = spectra_ref[0, window].astype(jnp.float32)
        imag = spectra_ref[1, window].astype(jnp.float32)
        power = jnp.sum(real * real + imag * imag, axis=0, keepdims=True) / bins
        live = alive_ref[window : window + 1, :].astype(jnp.float32)
        factor = live / jnp.sqrt(jnp.maximum(power, 0.5))
        rows_ref[row_of(0, window, windows)] = real * factor
        rows_ref[row_of(1, window, windows)] = imag * factor
    out_ref[...] = jnp.swapaxes(rows_ref[...], 0, 1).astype(jnp.bfloat16)
    for i in range(copies_ref.shape[0]):
        copies_ref[i] = out_ref[...]


def whiten(spectra, alive, copies):
    _, bins, windows, channels = spectra.shape
    by_window = jnp.swapaxes(spectra, 1, 2)
    return pl.pallas_call(
        lambda *refs: whiten_kernel(bins, *refs),
        out_shape=(
            jax.ShapeDtypeStruct((bins, 2 * windows, channels), jnp.bfloat16),
            jax.ShapeDtypeStruct((copies, bins, 2 * windows, channels), jnp.bfloat16),
        ),
        scratch_shapes=[pltpu.VMEM((2 * windows, bins, channels), jnp.float32)],
        name="whiten",
    )(by_window, alive)


def receiver_kernel(*refs):
    *in_refs, out_ref = refs
    slices, bins, rows, channels = in_refs[0].shape
    head = rows // 2 // TILE * TILE
    tail = rows - head
    half = (tail - head) // 2
    for f in range(bins):
        for piece in range(slices * len(in_refs)):
            block = in_refs[piece // slices][piece % slices, f]
            out_ref[f, piece, :, :channels] = block
            out_ref[f, piece, :head, channels:] = block[tail:]
            out_ref[f, piece, tail:, channels:] = -block[:head]
            mixed = block[head:tail].astype(jnp.float32)
            turned = jnp.concatenate((mixed[half:], -mixed[:half]), axis=0)
            out_ref[f, piece, head:tail, channels:] = turned.astype(jnp.bfloat16)


def receiver_pairs(receivers):
    slices, bins, rows, channels = receivers[0].shape
    total = slices * len(receivers)
    return pl.pallas_call(
        receiver_kernel,
        grid=(bins // STEP,),
        in_specs=[pl.BlockSpec((slices, STEP, rows, channels), lambda f: (0, f, 0, 0))] * len(receivers),
        out_specs=pl.BlockSpec((STEP, total, rows, 2 * channels), lambda f: (f, 0, 0, 0)),
        out_shape=jax.ShapeDtypeStruct((bins, total, rows, 2 * channels), jnp.bfloat16),
        name="receiver_pairs",
    )(*receivers)


def stack_kernel(parities, scale, place_ref, *refs):
    groups = refs[: len(parities)]
    pairs_ref, out_ref, even_ref, odd_ref = refs[len(parities) :]
    channels = groups[0].shape[3]
    parity_at = sum(group.shape[0] for group in groups)
    for f in range(out_ref.shape[1]):
        slot = 0
        for group, parity in zip(groups, parities):
            for i in range(group.shape[0]):
                held = odd_ref if parity[i] else even_ref
                held[f, place_ref[slot]] = group[i, f]
                slot += 1
        pairs = pairs_ref[f].reshape(-1, 2 * channels)
        for held, side in ((even_ref, place_ref[parity_at]), (odd_ref, 1 - place_ref[parity_at])):
            total = lax.dot_general(
                held[f].reshape(-1, channels),
                pairs,
                (((0,), (0,)), ((), ())),
                preferred_element_type=jnp.float32,
            )
            total = (total * scale).astype(jnp.bfloat16)
            at = pl.ds(pl.multiple_of(side * channels, channels), channels)
            out_ref[0, f, at, :] = total[:, :channels]
            out_ref[1, f, at, :] = total[:, channels:]


def stack(groups, parities, place, pairs, scale):
    bins, slices, rows, twice = pairs.shape
    channels = twice // 2
    return pl.pallas_call(
        lambda *refs: stack_kernel(parities, scale, *refs),
        grid=(bins // STACK_STEP,),
        in_specs=[pl.BlockSpec(memory_space=pltpu.SMEM)]
        + [pl.BlockSpec((g.shape[0], STACK_STEP, rows, channels), lambda f: (0, f, 0, 0)) for g in groups]
        + [pl.BlockSpec((STACK_STEP, slices, rows, twice), lambda f: (f, 0, 0, 0))],
        out_specs=pl.BlockSpec((2, STACK_STEP, 2 * channels, channels), lambda f: (0, f, 0, 0)),
        out_shape=jax.ShapeDtypeStruct((2, bins, 2 * channels, channels), jnp.bfloat16),
        scratch_shapes=[pltpu.VMEM((STACK_STEP, slices, rows, channels), jnp.bfloat16)] * 2,
        name="stack",
    )(place, *groups, pairs)


def body(spectra, alive):
    rows_n, cols_n = lax.axis_size("src"), lax.axis_size("rcv")
    length = cols_n // 2
    windows = spectra.shape[2] * rows_n

    def along(z_of, step):
        return z_of // length * length + (z_of % length + step) % length

    def shift(block, step):
        return lax.ppermute(block, "rcv", [(r, along(r, step)) for r in range(cols_n)])

    def trade(block):
        return lax.ppermute(block, "rcv", [(r, (r + length) % cols_n) for r in range(cols_n)])

    def deal(block, step):
        pairs = [
            (s * cols_n + 2 * d + o, d * cols_n + along(2 * s + o, step))
            for s in range(rows_n)
            for d in range(rows_n)
            for o in range(2)
        ]
        return lax.ppermute(block, ("src", "rcv"), pairs)

    def cross(block, bit):
        return lax.ppermute(block, "src", [(s, s ^ bit) for s in range(rows_n)])

    local, copies = whiten(spectra, alive, rows_n)
    dealt = [deal(local, step)[None] for step in (0, 5, -5)]
    receivers = (lax.all_to_all(copies, "src", 0, 0),)
    first = jnp.concatenate(dealt, axis=0)
    up, down, other = shift(first, 1), shift(first, -1), trade(first)
    up2, down2, far = shift(up, 1), shift(down, -1), shift(down[2:], -2)
    up2, pairs = lax.optimization_barrier((up2, receiver_pairs(receivers)))
    other_up, other_down = shift(other, 1), shift(other, -1)
    other_up2 = trade(jnp.concatenate((up2, far), axis=0))
    last = trade(down2)

    groups = (first, up, down, up2, down2, far, other, other_up, other_down, other_up2, last)
    own = lax.axis_index("rcv") // length
    z = lax.axis_index("rcv") % length
    offsets = OWN_SLOTS + NEIGHBOUR_SLOTS
    swaps = [i >= len(OWN_SLOTS) for i, group in enumerate(offsets) for _ in group]
    steps = [step % length for group in offsets for step in group]
    row = jnp.where(np.array(swaps), 1 - own, own)
    place = row * (rows_n // 2) + lax.rem(z + np.array(steps, np.int32), length) // 2
    place = jnp.append(place, z % 2).astype(jnp.int32)
    parities = tuple(tuple(step % 2 for step in group) for group in offsets)
    scale = 1.0 / float(windows) ** 0.5
    return stack(groups, parities, place, pairs, scale)


def solution(mesh):
    return jax.shard_map(
        body,
        mesh=mesh,
        in_specs=(P(None, None, "src", "rcv"), P("src", "rcv")),
        out_specs=P(None, None, "src", "rcv"),
        check_vma=False,
    )
```

```python
import jax
import jax.numpy as jnp
import numpy as np
from jax import lax
from jax.experimental import pallas as pl
from jax.experimental.pallas import tpu as pltpu
from jax.sharding import PartitionSpec as P

TILE = 8
STACK_STEP = 4
STEP = 2

OWN_SLOTS = ((0, -5, 5), (-1, -6, 4), (1, -4, 6), (-2, -7, 3), (2, -3, 7), (8,))
NEIGHBOUR_SLOTS = ((0, -5, 5), (-1, -6, 4), (1, -4, 6), (-2, -7, 3, 8), (2, -3, 7))


def row_of(part, window, windows):
    head = windows // TILE * TILE
    if window < head:
        return part * (2 * windows - head) + window
    return head + part * (windows - head) + window - head


def whiten_kernel(bins, spectra_ref, alive_ref, out_ref, copies_ref, rows_ref):
    windows = spectra_ref.shape[1]
    for window in range(windows):
        real = spectra_ref[0, window].astype(jnp.float32)
        imag = spectra_ref[1, window].astype(jnp.float32)
        power = jnp.sum(real * real + imag * imag, axis=0, keepdims=True) / bins
        live = alive_ref[window : window + 1, :].astype(jnp.float32)
        factor = live / jnp.sqrt(jnp.maximum(power, 0.5))
        rows_ref[row_of(0, window, windows)] = real * factor
        rows_ref[row_of(1, window, windows)] = imag * factor
    out_ref[...] = jnp.swapaxes(rows_ref[...], 0, 1).astype(jnp.bfloat16)
    for i in range(copies_ref.shape[0]):
        copies_ref[i] = out_ref[...]


def whiten(spectra, alive, copies):
    _, bins, windows, channels = spectra.shape
    by_window = jnp.swapaxes(spectra, 1, 2)
    return pl.pallas_call(
        lambda *refs: whiten_kernel(bins, *refs),
        out_shape=(
            jax.ShapeDtypeStruct((bins, 2 * windows, channels), jnp.bfloat16),
            jax.ShapeDtypeStruct((copies, bins, 2 * windows, channels), jnp.bfloat16),
        ),
        scratch_shapes=[pltpu.VMEM((2 * windows, bins, channels), jnp.float32)],
        name="whiten",
    )(by_window, alive)


def receiver_kernel(*refs):
    *in_refs, out_ref = refs
    slices, bins, rows, channels = in_refs[0].shape
    head = rows // 2 // TILE * TILE
    tail = rows - head
    half = (tail - head) // 2
    for f in range(bins):
        for piece in range(slices * len(in_refs)):
            block = in_refs[piece // slices][piece % slices, f]
            out_ref[f, piece, :, :channels] = block
            out_ref[f, piece, :head, channels:] = block[tail:]
            out_ref[f, piece, tail:, channels:] = -block[:head]
            mixed = block[head:tail].astype(jnp.float32)
            turned = jnp.concatenate((mixed[half:], -mixed[:half]), axis=0)
            out_ref[f, piece, head:tail, channels:] = turned.astype(jnp.bfloat16)


def receiver_pairs(receivers):
    slices, bins, rows, channels = receivers[0].shape
    total = slices * len(receivers)
    return pl.pallas_call(
        receiver_kernel,
        grid=(bins // STEP,),
        in_specs=[pl.BlockSpec((slices, STEP, rows, channels), lambda f: (0, f, 0, 0))] * len(receivers),
        out_specs=pl.BlockSpec((STEP, total, rows, 2 * channels), lambda f: (f, 0, 0, 0)),
        out_shape=jax.ShapeDtypeStruct((bins, total, rows, 2 * channels), jnp.bfloat16),
        name="receiver_pairs",
    )(*receivers)


def stack_kernel(parities, scale, place_ref, *refs):
    groups = refs[: len(parities)]
    pairs_ref, out_ref, even_ref, odd_ref = refs[len(parities) :]
    channels = groups[0].shape[3]
    parity_at = sum(group.shape[0] for group in groups)
    for f in range(out_ref.shape[1]):
        slot = 0
        for group, parity in zip(groups, parities):
            for i in range(group.shape[0]):
                held = odd_ref if parity[i] else even_ref
                held[f, place_ref[slot]] = group[i, f]
                slot += 1
        pairs = pairs_ref[f].reshape(-1, 2 * channels)
        for held, side in ((even_ref, place_ref[parity_at]), (odd_ref, 1 - place_ref[parity_at])):
            total = lax.dot_general(
                held[f].reshape(-1, channels),
                pairs,
                (((0,), (0,)), ((), ())),
                preferred_element_type=jnp.float32,
            )
            total = (total * scale).astype(jnp.bfloat16)
            at = pl.ds(pl.multiple_of(side * channels, channels), channels)
            out_ref[0, f, at, :] = total[:, :channels]
            out_ref[1, f, at, :] = total[:, channels:]


def stack(groups, parities, place, pairs, scale):
    bins, slices, rows, twice = pairs.shape
    channels = twice // 2
    return pl.pallas_call(
        lambda *refs: stack_kernel(parities, scale, *refs),
        grid=(bins // STACK_STEP,),
        in_specs=[pl.BlockSpec(memory_space=pltpu.SMEM)]
        + [pl.BlockSpec((g.shape[0], STACK_STEP, rows, channels), lambda f: (0, f, 0, 0)) for g in groups]
        + [pl.BlockSpec((STACK_STEP, slices, rows, twice), lambda f: (f, 0, 0, 0))],
        out_specs=pl.BlockSpec((2, STACK_STEP, 2 * channels, channels), lambda f: (0, f, 0, 0)),
        out_shape=jax.ShapeDtypeStruct((2, bins, 2 * channels, channels), jnp.bfloat16),
        scratch_shapes=[pltpu.VMEM((STACK_STEP, slices, rows, channels), jnp.bfloat16)] * 2,
        name="stack",
    )(place, *groups, pairs)


def body(spectra, alive):
    rows_n, cols_n = lax.axis_size("src"), lax.axis_size("rcv")
    length = cols_n // 2
    windows = spectra.shape[2] * rows_n

    def along(z_of, step):
        return z_of // length * length + (z_of % length + step) % length

    def shift(block, step):
        return lax.ppermute(block, "rcv", [(r, along(r, step)) for r in range(cols_n)])

    def trade(block):
        return lax.ppermute(block, "rcv", [(r, (r + length) % cols_n) for r in range(cols_n)])

    def deal(block, step):
        pairs = [
            (s * cols_n + 2 * d + o, d * cols_n + along(2 * s + o, step))
            for s in range(rows_n)
            for d in range(rows_n)
            for o in range(2)
        ]
        return lax.ppermute(block, ("src", "rcv"), pairs)

    def cross(block, bit):
        return lax.ppermute(block, "src", [(s, s ^ bit) for s in range(rows_n)])

    local, copies = whiten(spectra, alive, rows_n)
    dealt = [deal(local, step)[None] for step in (0, 5, -5)]
    receivers = (lax.all_to_all(copies, "src", 0, 0),)
    first = jnp.concatenate(dealt, axis=0)
    up, down, other = shift(first, 1), shift(first, -1), trade(first)
    up2, down2, far = shift(up, 1), shift(down, -1), shift(up[1:2], 2)
    up2, pairs = lax.optimization_barrier((up2, receiver_pairs(receivers)))
    other_up, other_down = shift(other, 1), shift(other, -1)
    other_up2 = trade(jnp.concatenate((up2, far), axis=0))
    last = trade(down2)

    groups = (first, up, down, up2, down2, far, other, other_up, other_down, other_up2, last)
    own = lax.axis_index("rcv") // length
    z = lax.axis_index("rcv") % length
    offsets = OWN_SLOTS + NEIGHBOUR_SLOTS
    swaps = [i >= len(OWN_SLOTS) for i, group in enumerate(offsets) for _ in group]
    steps = [step % length for group in offsets for step in group]
    row = jnp.where(np.array(swaps), 1 - own, own)
    place = row * (rows_n // 2) + lax.rem(z + np.array(steps, np.int32), length) // 2
    place = jnp.append(place, z % 2).astype(jnp.int32)
    parities = tuple(tuple(step % 2 for step in group) for group in offsets)
    scale = 1.0 / float(windows) ** 0.5
    return stack(groups, parities, place, pairs, scale)


def solution(mesh):
    return jax.shard_map(
        body,
        mesh=mesh,
        in_specs=(P(None, None, "src", "rcv"), P("src", "rcv")),
        out_specs=P(None, None, "src", "rcv"),
        check_vma=False,
    )
```

```python
import jax
import jax.numpy as jnp
import numpy as np
from jax import lax
from jax.experimental import pallas as pl
from jax.experimental.pallas import tpu as pltpu
from jax.sharding import PartitionSpec as P

TILE = 8
STACK_STEP = 4
STEP = 4

OWN_SLOTS = ((0, -5, 5), (-1, -6, 4), (1, -4, 6), (-2, -7, 3), (2, -3, 7), (8,))
NEIGHBOUR_SLOTS = ((0, -5, 5), (-1, -6, 4), (1, -4, 6), (-2, -7, 3, 8), (2, -3, 7))


def row_of(part, window, windows):
    head = windows // TILE * TILE
    if window < head:
        return part * (2 * windows - head) + window
    return head + part * (windows - head) + window - head


def whiten_kernel(bins, spectra_ref, alive_ref, out_ref, copies_ref, rows_ref):
    windows = spectra_ref.shape[1]
    for window in range(windows):
        real = spectra_ref[0, window].astype(jnp.float32)
        imag = spectra_ref[1, window].astype(jnp.float32)
        power = jnp.sum(real * real + imag * imag, axis=0, keepdims=True) / bins
        live = alive_ref[window : window + 1, :].astype(jnp.float32)
        factor = live / jnp.sqrt(jnp.maximum(power, 0.5))
        rows_ref[row_of(0, window, windows)] = real * factor
        rows_ref[row_of(1, window, windows)] = imag * factor
    out_ref[...] = jnp.swapaxes(rows_ref[...], 0, 1).astype(jnp.bfloat16)
    for i in range(copies_ref.shape[0]):
        copies_ref[i] = out_ref[...]


def whiten(spectra, alive, copies):
    _, bins, windows, channels = spectra.shape
    by_window = jnp.swapaxes(spectra, 1, 2)
    return pl.pallas_call(
        lambda *refs: whiten_kernel(bins, *refs),
        out_shape=(
            jax.ShapeDtypeStruct((bins, 2 * windows, channels), jnp.bfloat16),
            jax.ShapeDtypeStruct((copies, bins, 2 * windows, channels), jnp.bfloat16),
        ),
        scratch_shapes=[pltpu.VMEM((2 * windows, bins, channels), jnp.float32)],
        name="whiten",
    )(by_window, alive)


def receiver_kernel(*refs):
    *in_refs, out_ref = refs
    slices, bins, rows, channels = in_refs[0].shape
    head = rows // 2 // TILE * TILE
    tail = rows - head
    half = (tail - head) // 2
    for f in range(bins):
        for piece in range(slices * len(in_refs)):
            block = in_refs[piece // slices][piece % slices, f]
            out_ref[f, piece, :, :channels] = block
            out_ref[f, piece, :head, channels:] = block[tail:]
            out_ref[f, piece, tail:, channels:] = -block[:head]
            mixed = block[head:tail].astype(jnp.float32)
            turned = jnp.concatenate((mixed[half:], -mixed[:half]), axis=0)
            out_ref[f, piece, head:tail, channels:] = turned.astype(jnp.bfloat16)


def receiver_pairs(receivers):
    slices, bins, rows, channels = receivers[0].shape
    total = slices * len(receivers)
    return pl.pallas_call(
        receiver_kernel,
        grid=(bins // STEP,),
        in_specs=[pl.BlockSpec((slices, STEP, rows, channels), lambda f: (0, f, 0, 0))] * len(receivers),
        out_specs=pl.BlockSpec((STEP, total, rows, 2 * channels), lambda f: (f, 0, 0, 0)),
        out_shape=jax.ShapeDtypeStruct((bins, total, rows, 2 * channels), jnp.bfloat16),
        name="receiver_pairs",
    )(*receivers)


def stack_kernel(parities, scale, place_ref, *refs):
    groups = refs[: len(parities)]
    pairs_ref, out_ref, even_ref, odd_ref = refs[len(parities) :]
    channels = groups[0].shape[3]
    parity_at = sum(group.shape[0] for group in groups)
    for f in range(out_ref.shape[1]):
        slot = 0
        for group, parity in zip(groups, parities):
            for i in range(group.shape[0]):
                held = odd_ref if parity[i] else even_ref
                held[f, place_ref[slot]] = group[i, f]
                slot += 1
        pairs = pairs_ref[f].reshape(-1, 2 * channels)
        for held, side in ((even_ref, place_ref[parity_at]), (odd_ref, 1 - place_ref[parity_at])):
            total = lax.dot_general(
                held[f].reshape(-1, channels),
                pairs,
                (((0,), (0,)), ((), ())),
                preferred_element_type=jnp.float32,
            )
            total = (total * scale).astype(jnp.bfloat16)
            at = pl.ds(pl.multiple_of(side * channels, channels), channels)
            out_ref[0, f, at, :] = total[:, :channels]
            out_ref[1, f, at, :] = total[:, channels:]


def stack(groups, parities, place, pairs, scale):
    bins, slices, rows, twice = pairs.shape
    channels = twice // 2
    return pl.pallas_call(
        lambda *refs: stack_kernel(parities, scale, *refs),
        grid=(bins // STACK_STEP,),
        in_specs=[pl.BlockSpec(memory_space=pltpu.SMEM)]
        + [pl.BlockSpec((g.shape[0], STACK_STEP, rows, channels), lambda f: (0, f, 0, 0)) for g in groups]
        + [pl.BlockSpec((STACK_STEP, slices, rows, twice), lambda f: (f, 0, 0, 0))],
        out_specs=pl.BlockSpec((2, STACK_STEP, 2 * channels, channels), lambda f: (0, f, 0, 0)),
        out_shape=jax.ShapeDtypeStruct((2, bins, 2 * channels, channels), jnp.bfloat16),
        scratch_shapes=[pltpu.VMEM((STACK_STEP, slices, rows, channels), jnp.bfloat16)] * 2,
        name="stack",
    )(place, *groups, pairs)


def body(spectra, alive):
    rows_n, cols_n = lax.axis_size("src"), lax.axis_size("rcv")
    length = cols_n // 2
    windows = spectra.shape[2] * rows_n

    def along(z_of, step):
        return z_of // length * length + (z_of % length + step) % length

    def shift(block, step):
        return lax.ppermute(block, "rcv", [(r, along(r, step)) for r in range(cols_n)])

    def trade(block):
        return lax.ppermute(block, "rcv", [(r, (r + length) % cols_n) for r in range(cols_n)])

    def deal(block, step):
        pairs = [
            (s * cols_n + 2 * d + o, d * cols_n + along(2 * s + o, step))
            for s in range(rows_n)
            for d in range(rows_n)
            for o in range(2)
        ]
        return lax.ppermute(block, ("src", "rcv"), pairs)

    def cross(block, bit):
        return lax.ppermute(block, "src", [(s, s ^ bit) for s in range(rows_n)])

    local, copies = whiten(spectra, alive, rows_n)
    dealt = [deal(local, step)[None] for step in (0, 5, -5)]
    receivers = (lax.all_to_all(copies, "src", 0, 0),)
    first = jnp.concatenate(dealt, axis=0)
    up, down, other = shift(first, 1), shift(first, -1), trade(first)
    up2, down2, far = shift(up, 1), shift(down, -1), shift(up[1:2], 2)
    up2, pairs = lax.optimization_barrier((up2, receiver_pairs(receivers)))
    other_up, other_down = shift(other, 1), shift(other, -1)
    other_up2 = trade(jnp.concatenate((up2, far), axis=0))
    last = trade(down2)

    groups = (first, up, down, up2, down2, far, other, other_up, other_down, other_up2, last)
    own = lax.axis_index("rcv") // length
    z = lax.axis_index("rcv") % length
    offsets = OWN_SLOTS + NEIGHBOUR_SLOTS
    swaps = [i >= len(OWN_SLOTS) for i, group in enumerate(offsets) for _ in group]
    steps = [step % length for group in offsets for step in group]
    row = jnp.where(np.array(swaps), 1 - own, own)
    place = row * (rows_n // 2) + lax.rem(z + np.array(steps, np.int32), length) // 2
    place = jnp.append(place, z % 2).astype(jnp.int32)
    parities = tuple(tuple(step % 2 for step in group) for group in offsets)
    scale = 1.0 / float(windows) ** 0.5
    return stack(groups, parities, place, pairs, scale)


def solution(mesh):
    return jax.shard_map(
        body,
        mesh=mesh,
        in_specs=(P(None, None, "src", "rcv"), P("src", "rcv")),
        out_specs=P(None, None, "src", "rcv"),
        check_vma=False,
    )
```
